512 devices in a mesh: pulse: 8 (over x, core), range: 64 (over z, y).
Axes of the slice: x: 4, y: 8, z: 8, core: 2. Of those that a mesh axis runs over, the one named last changes fastest.
Arguments:
- echoes: bfloat16 [2, 2048, 32768], P(None, ('pulse', 'range')), may hold values from -6 to 6
- range_filter: float32 [2, 32768], replicated, may hold values from -6 to 6
- shift_table: int32 [32768], replicated, may hold values from -12 to 12
- tap_table: int32 [32768], replicated, may hold values from 0 to 15
- kernels: float32 [16, 8], replicated, may hold values from -2 to 2
- tail_lengths: int32 [256], P('range'), may hold values from 32 to 128, as said below
- azimuth_rate: float32 [32768], P('range'), may hold values from 0.5 to 4
Outputs:
- focused: bfloat16 [2, 2048, 32768], P(None, 'pulse', 'range')
The draws below stay inside these ranges and needn't reach their ends.
Inputs may be any that keep to these rules, and one draw needn't show every extreme that they name: `tail_lengths`: some range block has a tail of exactly 128 pulses and some of exactly 32.
All inputs are finite; a program needn't handle non-finite values.
Results may differ from the reference program's by a relative error of at most 0.0099.
Values may be sent and summed in bfloat16 or wider, within the bound.
A program may use at most 64 MiB of HBM per device.

```python
import math
import jax
import jax.numpy as jnp
from jax import lax

RA = 256
RB = 128
N = 32768
PG = 256
PULSES = 2048
TMAX = 128
SH = 12
HW = 16
TAPS = 8
NK = 16
RBLK = 128
N_PULSE = 8


def draw_tail_lengths(key, part):
    block_count = N // RBLK
    first_key = jax.random.fold_in(key, 11)
    second_key = jax.random.fold_in(key, 23)
    values = jax.random.randint(first_key, (block_count,), TMAX // 4, TMAX + 1)
    places = jax.random.permutation(second_key, block_count)
    values = values.at[places[0]].set(TMAX)
    values = values.at[places[1]].set(TMAX // 4)
    return values.astype(jnp.int32)


def with_ends(values, stream_key, smallest, top_value):
    longest = values.shape.index(max(values.shape))
    spots = []
    for shift in (0, 1):
        where = [jax.random.randint(jax.random.fold_in(stream_key, axis), (), 0, length) for axis, length in enumerate(values.shape)]
        where[longest] = (where[longest] + shift) % values.shape[longest]
        spots.append(tuple(where))
    return values.at[spots[0]].set(smallest).at[spots[1]].set(top_value)


def levels(stream_key, extent, split, smallest, largest):
    def one(dim, parts):
        steps = jax.random.uniform(jax.random.fold_in(jax.random.fold_in(stream_key, 6), dim), (parts,), jnp.float32, smallest / len(split), largest / len(split))
        return jnp.repeat(jnp.exp(steps), extent[dim] // parts).reshape((-1,) + (1,) * (len(extent) - dim - 1))

    level = one(*split[0])
    for cut in split[1:]:
        level = level * one(*cut)
    return level


def gaussian(rng, extent, spread, reach, split=(), held_as=jnp.bfloat16):
    values = jax.random.normal(rng, extent, jnp.float32) * spread
    if len(split) > 0:
        values = levels(rng, extent, split, -0.22, 0.18) * values
    return jnp.clip(values, min=-reach, max=reach).astype(held_as)


def setup_inputs(seed: int = 0) -> dict:
    streams_of = jax.random.split(jax.random.key(seed), 8)
    echoes = gaussian(streams_of[0], (2, PULSES, N), 1.0, 6.0, ((1, 512),))
    range_filter = gaussian(streams_of[1], (2, N), 1.0, 6.0, (), jnp.float32)
    shift_table = with_ends(jax.random.randint(streams_of[2], (N,), 0 - SH, SH + 1), jax.random.fold_in(streams_of[2], 1), 0 - SH, SH).astype(jnp.int32)
    tap_table = with_ends(jax.random.randint(streams_of[3], (N,), 0, NK), jax.random.fold_in(streams_of[3], 1), 0, NK - 1).astype(jnp.int32)
    kernels = gaussian(streams_of[4], (NK, TAPS), 0.35, 2.0, (), jnp.float32)
    tail_lengths = draw_tail_lengths(jax.random.fold_in(streams_of[7], 71), 0)
    azimuth_rate = jnp.clip(jnp.exp(math.log(4.0) - 2.0794415 * jax.random.uniform(streams_of[6], (N,), jnp.float32) ** levels(streams_of[6], (N,), ((0, 64),), -0.2, 0.2)), 0.5, 4.0)
    return dict(echoes=echoes, range_filter=range_filter, shift_table=shift_table, tap_table=tap_table, kernels=kernels, tail_lengths=tail_lengths, azimuth_rate=azimuth_rate)


def dft_table(row_count, col_count, seq_len):
    product = (jnp.arange(row_count, dtype=jnp.int32)[:, None] * jnp.arange(col_count, dtype=jnp.int32)[None, :]) % seq_len
    angle = product.astype(jnp.float32) * (-2.0 * math.pi / seq_len)
    return jnp.cos(angle), jnp.sin(angle)


def tables_bf16(row_count, col_count, seq_len):
    cos_part, sin_part = dft_table(row_count, col_count, seq_len)
    return cos_part.astype(jnp.bfloat16), sin_part.astype(jnp.bfloat16)


def complex_product(pattern, first_pair, second_pair):
    first_re = first_pair[0].astype(jnp.float32)
    first_im = first_pair[1].astype(jnp.float32)
    second_re = second_pair[0].astype(jnp.float32)
    second_im = second_pair[1].astype(jnp.float32)
    highest = lax.Precision.HIGHEST
    real_part = jnp.einsum(pattern, first_re, second_re, precision=highest) - jnp.einsum(pattern, first_im, second_im, precision=highest)
    imag_part = jnp.einsum(pattern, first_re, second_im, precision=highest) + jnp.einsum(pattern, first_im, second_re, precision=highest)
    return real_part, imag_part


def complex_scale(pair_in, factor_pair):
    real_part = pair_in[0] * factor_pair[0] - pair_in[1] * factor_pair[1]
    imag_part = pair_in[0] * factor_pair[1] + pair_in[1] * factor_pair[0]
    return jnp.stack([real_part, imag_part]).astype(jnp.bfloat16)


def compress(echoes, range_filter):
    pulses_dev = echoes.shape[1]
    bins_all = echoes.shape[2]
    planes = echoes.reshape(2, pulses_dev, RA, RB)
    first_re, first_im = tables_bf16(RA, RA, RA)
    second_re, second_im = tables_bf16(RB, RB, RB)
    twiddle = dft_table(RA, RB, bins_all)
    spectrum_gain = range_filter.reshape(2, RB, RA).transpose(0, 2, 1)
    section_out = complex_product("ka,pab->pkb", (first_re, first_im), (planes[0], planes[1]))
    section_out = complex_scale(section_out, twiddle)
    section_out = complex_product("pkb,bq->pkq", (section_out[0], section_out[1]), (second_re, second_im))
    section_out = complex_scale(section_out, (spectrum_gain[0], spectrum_gain[1]))
    section_out = complex_product("pkq,qb->pkb", (section_out[0], section_out[1]), (second_re, -second_im))
    section_out = complex_scale(section_out, (twiddle[0], -twiddle[1]))
    section_out = complex_product("ak,pkb->pab", (first_re, -first_im), (section_out[0], section_out[1]))
    result = jnp.stack([section_out[0], section_out[1]]) * (1.0 / bins_all)
    return result.astype(jnp.bfloat16).reshape(2, pulses_dev, bins_all)


def interpolate(padded, shifts, taps, kernels):
    bin_count = shifts.shape[0]
    onehot = (taps[:, None] == jnp.arange(NK, dtype=jnp.int32)[None, :]).astype(jnp.float32)
    weights = jnp.dot(onehot, kernels, precision=lax.Precision.HIGHEST)
    anchor = jnp.arange(bin_count, dtype=jnp.int32) + shifts + (HW - 3)
    summed = jnp.zeros((padded.shape[0], padded.shape[1], bin_count), jnp.float32)
    for offset in range(TAPS):
        summed = summed + padded[:, :, anchor + offset].astype(jnp.float32) * weights[:, offset]
    return summed.astype(jnp.bfloat16)


def azimuth(own_rows, tail_rows, tail_len, rates):
    inside = jnp.arange(TMAX, dtype=jnp.int32)[:, None] >= (TMAX - tail_len)[None, :]
    tail_rows = jnp.where(inside[None], tail_rows, jnp.zeros_like(tail_rows))
    sequence = jnp.concatenate([tail_rows, own_rows], axis=1)
    seq_len = sequence.shape[1]
    kept_rows = own_rows.shape[1]
    table_re, table_im = tables_bf16(seq_len, seq_len, seq_len)
    doppler = complex_product("fm,mr->fr", (table_re, table_im), (sequence[0], sequence[1]))
    centre = ((jnp.arange(seq_len, dtype=jnp.int32) + seq_len // 2) % seq_len - seq_len // 2).astype(jnp.float32)
    phases = rates[None, :] * (centre * centre)[:, None] * (1.0 / seq_len)
    doppler = complex_scale(doppler, (jnp.cos(phases), jnp.sin(phases)))
    first_row = seq_len - kept_rows
    result = complex_product("if,fr->ir", (table_re[first_row:], -table_im[first_row:]), (doppler[0], doppler[1]))
    return (jnp.stack([result[0], result[1]]) * (1.0 / seq_len)).astype(jnp.bfloat16)


def reference(echoes, range_filter, shift_table, tap_table, kernels, tail_lengths, azimuth_rate):
    stacked = echoes.reshape(2, N_PULSE, PG, N).transpose(1, 0, 2, 3)

    def prepare(group_rows):
        compressed = compress(group_rows, range_filter)
        padded = jnp.pad(compressed, ((0, 0), (0, 0), (HW, HW)))
        return interpolate(padded, shift_table, tap_table, kernels)

    migrated = lax.map(prepare, stacked)
    earlier = jnp.concatenate([jnp.zeros((1, 2, TMAX, N), jnp.bfloat16), migrated[:-1, :, PG - TMAX:, :]], axis=0)
    tail_len = jnp.repeat(tail_lengths, RBLK)

    def focus_group(inputs_pair):
        return azimuth(inputs_pair[0], inputs_pair[1], tail_len, azimuth_rate)

    focused = lax.map(focus_group, (migrated, earlier))
    return focused.transpose(1, 0, 2, 3).reshape(2, PULSES, N)
```

```python
import math

import jax
import jax.numpy as jnp
import numpy as np
from jax import lax
from jax.experimental import pallas as pl
from jax.experimental.pallas import tpu as pltpu
from jax.sharding import PartitionSpec as P

RA = 256
RB = 128
TMAX = 128
NK = 16
RBLK = 128
NR = 64
PD = 4
MSG = 40
F32 = jnp.float32
BF16 = jnp.bfloat16
MESH = pl.DeviceIdType.MESH


def table(rows, cols, length):
    prod = (np.asarray(rows)[:, None] * np.asarray(cols)[None, :]) % length
    angle = prod.astype(np.float32) * np.float32(-2.0 * math.pi / length)
    return np.cos(angle).astype(np.float32), np.sin(angle).astype(np.float32)


def bf(value):
    return np.asarray(value).astype(jnp.bfloat16)


def range_constants():
    ra = np.arange(RA)
    wr, wi = table(ra, ra, RA)
    first = bf(np.block([[wr, -wi], [wi, wr]]))
    vr, vi = table(np.arange(RB), np.arange(RB), RB)
    second = bf(np.block([[vr, vi], [-vi, vr]]))
    third = bf(np.block([[vr, -vi], [vi, vr]]))
    real = np.concatenate([wr, wi], 1)
    imag = np.concatenate([-wi, wr], 1)
    both = np.stack([real, imag])
    main = both.reshape(2, NR, 4, 2 * RA).transpose(1, 0, 2, 3).reshape(8 * NR, 2 * RA)
    zero = np.zeros((2, 1, 2 * RA), np.float32)
    right = np.concatenate([both[:, 4::4], zero], 1).reshape(2 * NR, 2 * RA)
    left = np.concatenate([zero, both[:, 3:-1:4]], 1).reshape(2 * NR, 2 * RA)
    inverse = bf(bf(np.concatenate([main, right, left], 0)).astype(np.float32) * np.float32(2.0**-15))
    tr, ti = table(ra, np.arange(RB), RA * RB)
    return first, second, third, inverse, np.stack([tr, ti])


def azimuth_constants():
    seq = 384
    half = seq // 2
    freq = np.concatenate([np.arange(half), [half], seq - np.arange(1, half)])
    tail = np.array([4 * s + p for p in range(PD) for s in range(NR // 2)])
    own = np.array([TMAX + 4 * s + p for p in range(PD) for s in range(NR)])
    rows = np.concatenate([own, tail])
    wr, wi = table(freq, rows, seq)
    no = own.size
    fr = [wr[:, :no], -wi[:, :no], wr[:, no:], -wi[:, no:]]
    fi = [wi[:, :no], wr[:, :no], wi[:, no:], wr[:, no:]]
    forward = bf(np.concatenate([np.concatenate(fr, 1), np.concatenate(fi, 1)], 0))
    out_rows = TMAX + np.arange(seq - TMAX)
    ur, ui = table(out_rows, freq, seq)
    inverse = bf(np.block([[ur, ui], [-ui, ur]]))
    return forward, inverse


def dot(a, b):
    return jnp.dot(a, b, preferred_element_type=F32)


def compress_kernel(x_ref, rf_ref, w1_ref, v2_ref, v3_ref, w6_ref, tw_ref, out_ref, xs, xb, gb, hs, es):
    for c in range(2):
        xs[c] = x_ref[c].astype(F32)
    for c in range(2):
        for p in range(PD):
            xb[c * RA : (c + 1) * RA, p * RB : (p + 1) * RB] = xs[c, pl.ds(p, RA, stride=PD), :].astype(BF16)
    for c in range(2):
        for h in range(2):
            part = rf_ref[pl.ds(2 * h + c, RB, stride=4), :]
            hs[c, h * RB : (h + 1) * RB, :] = part.T
    twr, twi = tw_ref[0], tw_ref[1]
    for u in range(2):
        s1 = dot(w1_ref[...], xb[:, 256 * u : 256 * (u + 1)])
        for v in range(2):
            p = 2 * u + v
            re = s1[:RA, v * RB : (v + 1) * RB]
            im = s1[RA:, v * RB : (v + 1) * RB]
            a = jnp.concatenate([re * twr - im * twi, re * twi + im * twr], axis=1).astype(BF16)
            t = dot(a, v2_ref[...])
            re, im = t[:, :RB], t[:, RB:]
            hr, hi = hs[0], hs[1]
            a = jnp.concatenate([re * hr - im * hi, re * hi + im * hr], axis=1).astype(BF16)
            t = dot(a, v3_ref[...])
            re, im = t[:, :RB], t[:, RB:]
            gb[:RA, p * RB : (p + 1) * RB] = (re * twr + im * twi).astype(BF16)
            gb[RA:, p * RB : (p + 1) * RB] = (im * twr - re * twi).astype(BF16)
    lane = lax.broadcasted_iota(jnp.int32, (2 * NR, RB), 1)
    for u in range(2):
        g = gb[:, 256 * u : 256 * (u + 1)]
        m = dot(w6_ref[: 8 * NR, :], g)
        e = dot(w6_ref[8 * NR :, :], g)
        parts = []
        for v in range(2):
            p = 2 * u + v
            parts.append(m[:, v * RB : (v + 1) * RB].reshape(NR, 8, RB))
            ev = e[:, v * RB : (v + 1) * RB]
            sel = jnp.where(lane < 64, ev[: 2 * NR], ev[2 * NR :])
            for c in range(2):
                es[pl.ds(2 * p + c, NR, stride=8), :] = sel[c * NR : (c + 1) * NR]
        out_ref[:, 16 * u : 16 * (u + 1), :] = jnp.concatenate(parts, axis=1).astype(BF16)
    out_ref[:, 32:40, :] = es[...].reshape(NR, 8, RB).astype(BF16)


def exchange_kernel(src_ref, dst_ref, send_sem, recv_sem, own_sem):
    me = lax.axis_index("range")
    barrier = pltpu.get_barrier_semaphore()

    def greet(i, carry):
        pl.semaphore_signal(barrier, inc=1, device_id={"range": lax.rem(me + i, NR)}, device_id_type=MESH)
        return carry

    lax.fori_loop(1, NR, greet, 0)
    own = pltpu.make_async_copy(src_ref.at[me], dst_ref.at[me], own_sem)
    own.start()
    pl.semaphore_wait(barrier, NR - 1)

    def copy(i):
        peer = lax.rem(me + i, NR)
        return pltpu.make_async_remote_copy(
            src_ref=src_ref.at[peer],
            dst_ref=dst_ref.at[me],
            send_sem=send_sem.at[i],
            recv_sem=recv_sem.at[i],
            device_id={"range": peer},
            device_id_type=MESH,
        )

    def send(i, carry):
        copy(i).start()
        return carry

    def finish(i, carry):
        copy(i).wait()
        return carry

    lax.fori_loop(1, NR, send, 0)
    own.wait()
    lax.fori_loop(1, NR, finish, 0)


def migrate_kernel(x_ref, shift_ref, tap_ref, kern_ref, out_ref, tail_ref, xs, yb, bm):
    xs[...] = x_ref[...].reshape(NR * MSG, RB).astype(F32)
    for c in range(2):
        for p in range(PD):
            rows = slice(c * 256 + p * NR, c * 256 + (p + 1) * NR)
            halo = xs[pl.ds(32 + 2 * p + c, NR, stride=MSG), :].astype(BF16)
            yb[rows, 0:RB] = halo
            yb[rows, 5 * RB : 6 * RB] = halo
            for j in range(4):
                block = xs[pl.ds(8 * p + 4 * c + j, NR, stride=MSG), :].astype(BF16)
                yb[rows, (j + 1) * RB : (j + 2) * RB] = block
    bm[...] = jnp.zeros_like(bm)
    taps = tap_ref[...]
    coef = jnp.zeros((8, 4 * RB), F32)
    for k in range(NK):
        coef = coef + jnp.where(taps == k, kern_ref[:, k : k + 1], 0.0)
    shifts = shift_ref[...]
    for j in range(4):
        row = lax.broadcasted_iota(jnp.int32, (160, RB), 0)
        col = lax.broadcasted_iota(jnp.int32, (160, RB), 1)
        lanes = slice(j * RB, (j + 1) * RB)
        tap = row - col - shifts[:, lanes] - 13
        part = jnp.zeros((160, RB), F32)
        for t in range(8):
            part = part + jnp.where(tap == t, coef[t : t + 1, lanes], 0.0)
        top = RB * (1 + j % 2) - 16
        bm[j // 2, top : top + 160, (j % 2) * RB : (j % 2 + 1) * RB] = part.astype(BF16)
    for u in range(2):
        got = dot(yb[:, 256 * u : 256 * u + 512], bm[u]).astype(BF16)
        cols = slice(256 * u, 256 * (u + 1))
        out_ref[:, cols] = got
        for c in range(2):
            for p in range(PD):
                tail_ref[c * 128 + p * 32 : c * 128 + (p + 1) * 32, cols] = got[
                    c * 256 + p * NR + 32 : c * 256 + (p + 1) * NR
                ]


def sincos(phase):
    turns = phase * (2.0 / math.pi)
    near = jnp.floor(turns + 0.5)
    z = (turns - near) * (math.pi / 2)
    z2 = z * z
    sin = z * (1.0 + z2 * (-1.0 / 6 + z2 * (1.0 / 120 + z2 * (-1.0 / 5040 + z2 * (1.0 / 362880)))))
    cos = 1.0 + z2 * (-0.5 + z2 * (1.0 / 24 + z2 * (-1.0 / 720 + z2 * (1.0 / 40320))))
    quad = near.astype(jnp.int32)
    odd = (quad & 1) == 1
    s = jnp.where(odd, cos, sin)
    c = jnp.where(odd, sin, cos)
    s = jnp.where((quad & 2) == 2, -s, s)
    c = jnp.where(((quad + 1) & 2) == 2, -c, c)
    return s, c


def azimuth_kernel(own_ref, tail_ref, len_ref, rate_ref, w_ref, u_ref, out_ref, zt, db):
    first = lax.axis_index("pulse") == 0
    row = lax.broadcasted_iota(jnp.int32, (TMAX, 256), 0)
    when = 4 * lax.rem(row, 32) + row // 32
    for u in range(2):
        cols = slice(256 * u, 256 * (u + 1))
        limit = jnp.where(first, 2 * TMAX, TMAX - len_ref[:, cols])
        inside = when >= limit
        for c in range(2):
            part = tail_ref[c * TMAX : (c + 1) * TMAX, cols].astype(F32)
            zt[c * TMAX : (c + 1) * TMAX, :] = jnp.where(inside, part, 0.0).astype(BF16)
        d = dot(w_ref[:, :512], own_ref[:, cols]) + dot(w_ref[:, 512:], zt[...])
        rate = rate_ref[:, cols]
        centre = lax.broadcasted_iota(jnp.int32, (192, 256), 0).astype(F32)
        s1, c1 = sincos(rate * (centre * centre) * (1.0 / 384))
        edge = lax.broadcasted_iota(jnp.int32, (8, 256), 0).astype(F32)
        edge = jnp.where(edge == 0.0, 192.0, edge)
        s2, c2 = sincos(rate * (edge * edge) * (1.0 / 384))
        for h in range(2):
            s = s1 if h == 0 else jnp.concatenate([s2, s1[8:]], axis=0)
            co = c1 if h == 0 else jnp.concatenate([c2, c1[8:]], axis=0)
            re = d[192 * h : 192 * (h + 1)]
            im = d[384 + 192 * h : 384 + 192 * (h + 1)]
            db[192 * h : 192 * (h + 1), :] = (re * co - im * s).astype(BF16)
            db[384 + 192 * h : 384 + 192 * (h + 1), :] = (re * s + im * co).astype(BF16)
        out = dot(u_ref[...], db[...]) * (1.0 / 384)
        out_ref[0, :, cols] = out[:256].astype(BF16)
        out_ref[1, :, cols] = out[256:].astype(BF16)


def vmem(count):
    return [pl.BlockSpec(memory_space=pltpu.VMEM)] * count


def per_device(echoes, range_filter, shift_table, tap_table, kernels, tail_lengths, azimuth_rate):
    bins = azimuth_rate.shape[0]
    x = echoes.reshape(2, PD, RA, RB).transpose(0, 2, 1, 3).reshape(2, RA * PD, RB)
    rf = range_filter.reshape(2, RA, RB).transpose(1, 0, 2).reshape(2 * RA, RB)
    w1, v2, v3, w6, tw = range_constants()
    sent = pl.pallas_call(
        compress_kernel,
        out_shape=jax.ShapeDtypeStruct((NR, MSG, RB), BF16),
        in_specs=vmem(7),
        out_specs=pl.BlockSpec(memory_space=pltpu.VMEM),
        scratch_shapes=[
            pltpu.VMEM((2, RA * PD, RB), F32),
            pltpu.VMEM((2 * RA, PD * RB), BF16),
            pltpu.VMEM((2 * RA, PD * RB), BF16),
            pltpu.VMEM((2, RA, RB), F32),
            pltpu.VMEM((8 * NR, RB), F32),
        ],
        name="compress",
    )(x, rf, w1, v2, v3, w6, tw)
    got = pl.pallas_call(
        exchange_kernel,
        out_shape=jax.ShapeDtypeStruct((NR, MSG, RB), BF16),
        in_specs=vmem(1),
        out_specs=pl.BlockSpec(memory_space=pltpu.VMEM),
        scratch_shapes=[
            pltpu.SemaphoreType.DMA((NR,)),
            pltpu.SemaphoreType.DMA((NR,)),
            pltpu.SemaphoreType.DMA,
        ],
        compiler_params=pltpu.CompilerParams(collective_id=0, has_side_effects=True),
        name="exchange",
    )(sent)
    start = lax.axis_index("range") * bins
    shifts = lax.dynamic_slice_in_dim(shift_table, start, bins, 0)[None]
    taps = lax.dynamic_slice_in_dim(tap_table, start, bins, 0)[None]
    own, tail = pl.pallas_call(
        migrate_kernel,
        out_shape=[jax.ShapeDtypeStruct((512, bins), BF16), jax.ShapeDtypeStruct((256, bins), BF16)],
        in_specs=vmem(4),
        out_specs=vmem(2),
        scratch_shapes=[
            pltpu.VMEM((NR * MSG, RB), F32),
            pltpu.VMEM((512, 6 * RB), BF16),
            pltpu.VMEM((2, 512, 256), BF16),
        ],
        name="migrate",
    )(got, shifts, taps, kernels.T)
    count = lax.axis_size("pulse")
    tail = lax.ppermute(tail, "pulse", [(i, i + 1) for i in range(count - 1)])
    w, u = azimuth_constants()
    lens = jnp.repeat(tail_lengths, RBLK)[None]
    return pl.pallas_call(
        azimuth_kernel,
        out_shape=jax.ShapeDtypeStruct((2, 256, bins), BF16),
        in_specs=vmem(6),
        out_specs=pl.BlockSpec(memory_space=pltpu.VMEM),
        scratch_shapes=[pltpu.VMEM((256, 256), BF16), pltpu.VMEM((768, 256), BF16)],
        name="azimuth",
    )(own, tail, lens, azimuth_rate[None], w, u)


def solution(mesh):
    in_specs = (P(None, ("pulse", "range"), None), P(), P(), P(), P(), P("range"), P("range"))
    return jax.shard_map(
        per_device, mesh=mesh, in_specs=in_specs, out_specs=P(None, "pulse", "range"), check_vma=False
    )
```

```python
import math

import jax
import jax.numpy as jnp
import numpy as np
from jax import lax
from jax.experimental import pallas as pl
from jax.experimental.pallas import tpu as pltpu
from jax.sharding import PartitionSpec as P

RA = 256
RB = 128
TMAX = 128
NK = 16
RBLK = 128
NR = 64
PD = 4
MSG = 40
F32 = jnp.float32
BF16 = jnp.bfloat16
MESH = pl.DeviceIdType.MESH


def table(rows, cols, length):
    prod = (np.asarray(rows)[:, None] * np.asarray(cols)[None, :]) % length
    angle = prod.astype(np.float32) * np.float32(-2.0 * math.pi / length)
    return np.cos(angle).astype(np.float32), np.sin(angle).astype(np.float32)


def bf(value):
    return np.asarray(value).astype(jnp.bfloat16)


def range_constants():
    ra = np.arange(RA)
    wr, wi = table(ra, ra, RA)
    vr, vi = table(np.arange(RB), np.arange(RB), RB)
    real = np.concatenate([wr, wi], 1)
    imag = np.concatenate([-wi, wr], 1)
    both = np.stack([real, imag])
    main = both.reshape(2, NR, 4, 2 * RA).transpose(1, 0, 2, 3).reshape(8 * NR, 2 * RA)
    zero = np.zeros((2, 1, 2 * RA), np.float32)
    right = np.concatenate([both[:, 4::4], zero], 1).reshape(2 * NR, 2 * RA)
    left = np.concatenate([zero, both[:, 3:-1:4]], 1).reshape(2 * NR, 2 * RA)
    inverse = bf(bf(np.concatenate([main, right, left], 0)).astype(np.float32) * np.float32(2.0**-15))
    tr, ti = table(ra, np.arange(RB), RA * RB)
    return bf(np.stack([wr, wi])), bf(np.stack([vr, vi])), inverse, np.stack([tr, ti])


def azimuth_constants():
    seq = 384
    half = seq // 2
    freq = np.concatenate([np.arange(half), [half], seq - np.arange(1, half)])
    tail = np.array([4 * s + p for p in range(PD) for s in range(NR // 2)])
    own = np.array([TMAX + 4 * s + p for p in range(PD) for s in range(NR)])
    rows = np.concatenate([own, tail])
    wr, wi = table(freq, rows, seq)
    no = own.size
    fr = [wr[:, :no], -wi[:, :no], wr[:, no:], -wi[:, no:]]
    fi = [wi[:, :no], wr[:, :no], wi[:, no:], wr[:, no:]]
    forward = bf(np.concatenate([np.concatenate(fr, 1), np.concatenate(fi, 1)], 0))
    out_rows = TMAX + np.arange(seq - TMAX)
    ur, ui = table(out_rows, freq, seq)
    inverse = bf(np.block([[ur, ui], [-ui, ur]]))
    return forward, inverse


def dot(a, b):
    return jnp.dot(a, b, preferred_element_type=F32)


def peer_order():
    def hops(offset):
        return sum(min(d, 8 - d) for d in offset)

    offsets = [(i // 8, i % 8) for i in range(1, NR)]
    return sorted(offsets, key=lambda o: -hops(o))


def sincos(phase):
    turns = phase * (2.0 / math.pi)
    near = jnp.floor(turns + 0.5)
    z = (turns - near) * (math.pi / 2)
    z2 = z * z
    sin = z * (1.0 + z2 * (-1.0 / 6 + z2 * (1.0 / 120 + z2 * (-1.0 / 5040 + z2 * (1.0 / 362880)))))
    cos = 1.0 + z2 * (-0.5 + z2 * (1.0 / 24 + z2 * (-1.0 / 720 + z2 * (1.0 / 40320))))
    quad = near.astype(jnp.int32)
    odd = (quad & 1) == 1
    s = jnp.where(odd, cos, sin)
    c = jnp.where(odd, sin, cos)
    s = jnp.where((quad & 2) == 2, -s, s)
    c = jnp.where(((quad + 1) & 2) == 2, -c, c)
    return s, c


def compress(x_ref, rf_ref, wc_ref, vc_ref, w6_ref, tw_ref, src, xs, xb, gb, hs, es, w1, v2, v3):
    for c in range(2):
        xs[c] = x_ref[c].astype(F32)
    wr, wi = wc_ref[0], wc_ref[1]
    w1[:RA, :RA] = wr
    w1[RA:, :RA] = wi
    w1[:RA, RA:] = (-wi.astype(F32)).astype(BF16)
    w1[RA:, RA:] = wr
    vr, vi = vc_ref[0], vc_ref[1]
    minus = (-vi.astype(F32)).astype(BF16)
    for ref, upper, lower in ((v2, vi, minus), (v3, minus, vi)):
        ref[:RB, :RB] = vr
        ref[:RB, RB:] = upper
        ref[RB:, :RB] = lower
        ref[RB:, RB:] = vr
    for c in range(2):
        for p in range(PD):
            xb[c * RA : (c + 1) * RA, p * RB : (p + 1) * RB] = xs[c, pl.ds(p, RA, stride=PD), :].astype(BF16)
    for c in range(2):
        for h in range(2):
            part = rf_ref[pl.ds(2 * h + c, RB, stride=4), :]
            hs[c, h * RB : (h + 1) * RB, :] = part.T
    twr, twi = tw_ref[0], tw_ref[1]
    for u in range(2):
        s1 = dot(w1[...], xb[:, 256 * u : 256 * (u + 1)])
        for v in range(2):
            p = 2 * u + v
            re = s1[:RA, v * RB : (v + 1) * RB]
            im = s1[RA:, v * RB : (v + 1) * RB]
            a = jnp.concatenate([re * twr - im * twi, re * twi + im * twr], axis=1).astype(BF16)
            t = dot(a, v2[...])
            re, im = t[:, :RB], t[:, RB:]
            hr, hi = hs[0], hs[1]
            a = jnp.concatenate([re * hr - im * hi, re * hi + im * hr], axis=1).astype(BF16)
            t = dot(a, v3[...])
            re, im = t[:, :RB], t[:, RB:]
            gb[:RA, p * RB : (p + 1) * RB] = (re * twr + im * twi).astype(BF16)
            gb[RA:, p * RB : (p + 1) * RB] = (im * twr - re * twi).astype(BF16)
    lane = lax.broadcasted_iota(jnp.int32, (2 * NR, RB), 1)
    for u in range(2):
        g = gb[:, 256 * u : 256 * (u + 1)]
        m = dot(w6_ref[: 8 * NR, :], g)
        e = dot(w6_ref[8 * NR :, :], g)
        parts = []
        for v in range(2):
            p = 2 * u + v
            parts.append(m[:, v * RB : (v + 1) * RB].reshape(NR, 8, RB))
            ev = e[:, v * RB : (v + 1) * RB]
            sel = jnp.where(lane < 64, ev[: 2 * NR], ev[2 * NR :])
            for c in range(2):
                es[pl.ds(2 * p + c, NR, stride=8), :] = sel[c * NR : (c + 1) * NR]
        src[:, 16 * u : 16 * (u + 1), :] = jnp.concatenate(parts, axis=1).astype(BF16)
    src[:, 32:40, :] = es[...].reshape(NR, 8, RB).astype(BF16)


def migration_matrix(me, shift_ref, tap_ref, kern_ref, bm):
    bm[...] = jnp.zeros_like(bm)
    for j in range(4):
        taps = tap_ref[pl.ds(4 * me + j, 1), :]
        shifts = shift_ref[pl.ds(4 * me + j, 1), :]
        coef = jnp.zeros((8, RB), F32)
        for k in range(NK):
            coef = coef + jnp.where(taps == k, kern_ref[:, k : k + 1], 0.0)
        row = lax.broadcasted_iota(jnp.int32, (160, RB), 0)
        col = lax.broadcasted_iota(jnp.int32, (160, RB), 1)
        tap = row - col - shifts - 13
        part = jnp.zeros((160, RB), F32)
        for t in range(8):
            part = part + jnp.where(tap == t, coef[t : t + 1, :], 0.0)
        top = RB * (1 + j % 2) - 16
        bm[j // 2, top : top + 160, (j % 2) * RB : (j % 2 + 1) * RB] = part.astype(BF16)


def phase_tables(rate_ref, ph, edges):
    for u in range(2):
        cols = slice(256 * u, 256 * (u + 1))
        rate = rate_ref[:, cols]
        centre = lax.broadcasted_iota(jnp.int32, (192, 256), 0).astype(F32)
        ph[0, :, cols], ph[1, :, cols] = sincos(rate * (centre * centre) * (1.0 / 384))
        edge = lax.broadcasted_iota(jnp.int32, (8, 256), 0).astype(F32)
        edge = jnp.where(edge == 0.0, 192.0, edge)
        edges[0, :, cols], edges[1, :, cols] = sincos(rate * (edge * edge) * (1.0 / 384))


def gather_blocks(got, xs, yb):
    xs[...] = got[...].reshape(NR * MSG, RB).astype(F32)
    for c in range(2):
        for p in range(PD):
            rows = slice(c * 256 + p * NR, c * 256 + (p + 1) * NR)
            halo = xs[pl.ds(32 + 2 * p + c, NR, stride=MSG), :].astype(BF16)
            yb[rows, 0:RB] = halo
            yb[rows, 5 * RB : 6 * RB] = halo
            for j in range(4):
                block = xs[pl.ds(8 * p + 4 * c + j, NR, stride=MSG), :].astype(BF16)
                yb[rows, (j + 1) * RB : (j + 2) * RB] = block


def focus_kernel(
    x_ref, rf_ref, shift_ref, tap_ref, kern_ref, len_ref, rate_ref,
    wc_ref, vc_ref, w6_ref, tw_ref, w_ref, u_ref, out_ref,
    src, got, xs, xb, gb, hs, es, w1, v2, v3, xr, yb, bm, ph, edges, mig, tsrc, tgot, zt, dd, db,
    send_sem, recv_sem, own_sem, tail_send, tail_recv,
):
    me = lax.axis_index("range")
    group = lax.axis_index("pulse")
    z, y = me // 8, lax.rem(me, 8)
    order = peer_order()
    ahead, behind = lax.rem(group + 1, 8), lax.rem(group + 7, 8)
    barrier = pltpu.get_barrier_semaphore()

    def peer_of(offset):
        return lax.rem(z + offset[0], 8) * 8 + lax.rem(y + offset[1], 8)

    for offset in order:
        pl.semaphore_signal(barrier, inc=1, device_id={"range": peer_of(offset)}, device_id_type=MESH)
    for other in (ahead, behind):
        pl.semaphore_signal(barrier, inc=1, device_id={"pulse": other}, device_id_type=MESH)
    compress(x_ref, rf_ref, wc_ref, vc_ref, w6_ref, tw_ref, src, xs, xb, gb, hs, es, w1, v2, v3)
    own = pltpu.make_async_copy(src.at[me], got.at[me], own_sem)
    own.start()
    pl.semaphore_wait(barrier, NR + 1)
    copies = []
    for i, offset in enumerate(order):
        peer = peer_of(offset)
        copy = pltpu.make_async_remote_copy(
            src_ref=src.at[peer],
            dst_ref=got.at[me],
            send_sem=send_sem.at[i],
            recv_sem=recv_sem.at[i],
            device_id={"range": peer},
            device_id_type=MESH,
        )
        copy.start()
        copies.append(copy)
    migration_matrix(me, shift_ref, tap_ref, kern_ref, bm)
    phase_tables(rate_ref, ph, edges)
    own.wait()
    for copy in copies:
        copy.wait()
    gather_blocks(got, xr, yb)
    tails = []
    for u in range(2):
        cols = slice(256 * u, 256 * (u + 1))
        part = dot(yb[:, 256 * u : 256 * u + 512], bm[u]).astype(BF16)
        mig[:, cols] = part
        for c in range(2):
            for p in range(PD):
                first = c * 256 + p * NR + 32
                tsrc[u, c * TMAX + p * 32 : c * TMAX + (p + 1) * 32, :] = part[first : first + 32]
        copy = pltpu.make_async_remote_copy(
            src_ref=tsrc.at[u],
            dst_ref=tgot.at[u],
            send_sem=tail_send.at[u],
            recv_sem=tail_recv.at[u],
            device_id={"pulse": ahead},
            device_id_type=MESH,
        )
        copy.start()
        tails.append(copy)
    for u in range(2):
        dd[u] = dot(w_ref[:, :512], mig[:, 256 * u : 256 * (u + 1)])
    row = lax.broadcasted_iota(jnp.int32, (TMAX, 256), 0)
    when = 4 * lax.rem(row, 32) + row // 32
    for u in range(2):
        cols = slice(256 * u, 256 * (u + 1))
        limit = jnp.where(group == 0, 2 * TMAX, TMAX - len_ref[:, cols])
        inside = when >= limit
        tails[u].wait()
        for c in range(2):
            part = tgot[u, c * TMAX : (c + 1) * TMAX, :].astype(F32)
            zt[c * TMAX : (c + 1) * TMAX, :] = jnp.where(inside, part, 0.0).astype(BF16)
        d = dd[u] + dot(w_ref[:, 512:], zt[...])
        for h in range(2):
            s, co = ph[0, :, cols], ph[1, :, cols]
            if h == 1:
                s = jnp.concatenate([edges[0, :, cols], s[8:]], axis=0)
                co = jnp.concatenate([edges[1, :, cols], co[8:]], axis=0)
            re = d[192 * h : 192 * (h + 1)]
            im = d[384 + 192 * h : 384 + 192 * (h + 1)]
            db[192 * h : 192 * (h + 1), :] = (re * co - im * s).astype(BF16)
            db[384 + 192 * h : 384 + 192 * (h + 1), :] = (re * s + im * co).astype(BF16)
        out = dot(u_ref[...], db[...]) * (1.0 / 384)
        out_ref[0, :, cols] = out[:256].astype(BF16)
        out_ref[1, :, cols] = out[256:].astype(BF16)


def per_device(echoes, range_filter, shift_table, tap_table, kernels, tail_lengths, azimuth_rate):
    bins = azimuth_rate.shape[0]
    x = echoes.reshape(2, PD, RA, RB).transpose(0, 2, 1, 3).reshape(2, RA * PD, RB)
    rf = range_filter.reshape(2, RA, RB).transpose(1, 0, 2).reshape(2 * RA, RB)
    wc, vc, w6, tw = range_constants()
    w, u = azimuth_constants()
    lens = jnp.repeat(tail_lengths, RBLK)[None]
    operands = (
        x, rf, shift_table.reshape(RA, RB), tap_table.reshape(RA, RB), kernels.T, lens, azimuth_rate[None],
        wc, vc, w6, tw, w, u,
    )
    return pl.pallas_call(
        focus_kernel,
        out_shape=jax.ShapeDtypeStruct((2, 256, bins), BF16),
        in_specs=[pl.BlockSpec(memory_space=pltpu.VMEM)] * len(operands),
        out_specs=pl.BlockSpec(memory_space=pltpu.VMEM),
        scratch_shapes=[
            pltpu.VMEM((NR, MSG, RB), BF16),
            pltpu.VMEM((NR, MSG, RB), BF16),
            pltpu.VMEM((2, RA * PD, RB), F32),
            pltpu.VMEM((2 * RA, PD * RB), BF16),
            pltpu.VMEM((2 * RA, PD * RB), BF16),
            pltpu.VMEM((2, RA, RB), F32),
            pltpu.VMEM((8 * NR, RB), F32),
            pltpu.VMEM((2 * RA, 2 * RA), BF16),
            pltpu.VMEM((2 * RB, 2 * RB), BF16),
            pltpu.VMEM((2 * RB, 2 * RB), BF16),
            pltpu.VMEM((NR * MSG, RB), F32),
            pltpu.VMEM((512, 6 * RB), BF16),
            pltpu.VMEM((2, 512, 256), BF16),
            pltpu.VMEM((2, 192, bins), F32),
            pltpu.VMEM((2, 8, bins), F32),
            pltpu.VMEM((512, bins), BF16),
            pltpu.VMEM((2, 2 * TMAX, 256), BF16),
            pltpu.VMEM((2, 2 * TMAX, 256), BF16),
            pltpu.VMEM((2 * TMAX, 256), BF16),
            pltpu.VMEM((2, 768, 256), F32),
            pltpu.VMEM((768, 256), BF16),
            pltpu.SemaphoreType.DMA((NR,)),
            pltpu.SemaphoreType.DMA((NR,)),
            pltpu.SemaphoreType.DMA,
            pltpu.SemaphoreType.DMA((2,)),
            pltpu.SemaphoreType.DMA((2,)),
        ],
        compiler_params=pltpu.CompilerParams(collective_id=0, has_side_effects=True),
        name="focus",
    )(*operands)


def solution(mesh):
    in_specs = (P(None, ("pulse", "range"), None), P(), P(), P(), P(), P("range"), P("range"))
    return jax.shard_map(
        per_device, mesh=mesh, in_specs=in_specs, out_specs=P(None, "pulse", "range"), check_vma=False
    )
```
